32 devices in a mesh: region: 16 (over z, y, core), panel: 2 (over x).
Axes of the slice: x: 2, y: 2, z: 4, core: 2. Of those that a mesh axis runs over, the one named last changes fastest.
Arguments:
- multipliers: bfloat16 [16, 4096, 512], P('region', 'panel'), may hold values from -6 to 6
- flexibility: bfloat16 [16, 4096, 4096], P('region', 'panel'), as said below
- interface_sizes: int32 [16], P('region'), may hold values from 1024 to 4096, as said below
- send_rows: int32 [16, 2, 1536], replicated, may hold values from 0 to 4095, as said below
- recv_rows: int32 [16, 2, 1536], P('region'), may hold values from 0 to 4095, as said below
- recv_pos: int32 [16, 2, 1536], P('region'), may hold values from 0 to 1534
- recv_weight: float32 [16, 2, 1536], P('region'), may hold values from 0 to 1
Outputs:
- dual_image: float32 [16, 4096, 512], P('region', None, 'panel')
The draws below stay inside these ranges and needn't reach their ends.
Inputs may be any that keep to these rules, and one draw needn't show every extreme that they name: `flexibility`: each region's matrix is symmetric. `interface_sizes`: A multiple of 128. `send_rows`: every entry of region r is below interface_sizes[r]; side 0 faces region r - 1 and side 1 region r + 1 around the loop; rows may repeat. `recv_rows`: every entry of region r is below interface_sizes[r]; rows may repeat.
All inputs are finite; a program needn't handle non-finite values.
Results may differ from the reference program's by a relative error of at most 0.0029.
Values may be sent and summed in bfloat16 or wider, within the bound.
No kernel may reach another device: no remote copies, remote signals or barrier semaphores. Data moves between devices by JAX's collectives and lax.ppermute only.
A program may use at most 128 MiB of HBM per device.

```python
import math
import jax
import jax.numpy as jnp
from jax import lax

M = 4096
K = 512
S = 1536
PAD = 128
REGIONS = 16


def draw_interface_sizes(key, part):
    sized_key = jax.random.fold_in(key, 11)
    first_key, second_key = jax.random.split(sized_key)
    blocks = M // PAD
    lowest = blocks // 4
    drawn = jax.random.randint(first_key, (REGIONS,), lowest, blocks + 1)
    ranking = jax.random.permutation(second_key, REGIONS)
    drawn = jnp.where(ranking == 0, blocks, drawn)
    drawn = jnp.where(ranking == 1, lowest, drawn)
    return (drawn * PAD).astype(jnp.int32)


def draw_send_rows(key, part):

    def listed(salt):
        sizes_now = draw_interface_sizes(key, part)
        list_key = jax.random.fold_in(key, salt)
        first_key, second_key, third_key = jax.random.split(list_key, 3)
        drawn = jax.random.randint(first_key, (REGIONS, 2, S), 0, 1073741824)
        rows_out = drawn % sizes_now[:, None, None]
        forced_at = jax.random.randint(second_key, (REGIONS, 2, 1), 0, S)
        stride = jax.random.randint(third_key, (REGIONS, 2, 1), 1, S)
        other_at = (forced_at + stride) % S
        slot_index = jnp.arange(S, dtype=jnp.int32)[None, None, :]
        rows_out = jnp.where(slot_index == forced_at, sizes_now[:, None, None] - 1, rows_out)
        rows_out = jnp.where(slot_index == other_at, 0, rows_out)
        return rows_out.astype(jnp.int32)
    return listed(21)


def draw_recv_rows(key, part):

    def listed(salt):
        sizes_now = draw_interface_sizes(key, part)
        list_key = jax.random.fold_in(key, salt)
        first_key, second_key, third_key = jax.random.split(list_key, 3)
        drawn = jax.random.randint(first_key, (REGIONS, 2, S), 0, 1073741824)
        rows_out = drawn % sizes_now[:, None, None]
        forced_at = jax.random.randint(second_key, (REGIONS, 2, 1), 0, S)
        stride = jax.random.randint(third_key, (REGIONS, 2, 1), 1, S)
        other_at = (forced_at + stride) % S
        slot_index = jnp.arange(S, dtype=jnp.int32)[None, None, :]
        rows_out = jnp.where(slot_index == forced_at, sizes_now[:, None, None] - 1, rows_out)
        rows_out = jnp.where(slot_index == other_at, 0, rows_out)
        return rows_out.astype(jnp.int32)
    return listed(22)


def draw_recv_pos(key, part):
    pos_key = jax.random.fold_in(key, 31)
    first_key, second_key, third_key = jax.random.split(pos_key, 3)
    drawn = jax.random.randint(first_key, (REGIONS, 2, S), 0, S - 1)
    forced_at = jax.random.randint(second_key, (REGIONS, 2, 1), 0, S)
    stride = jax.random.randint(third_key, (REGIONS, 2, 1), 1, S)
    other_at = (forced_at + stride) % S
    slot_index = jnp.arange(S, dtype=jnp.int32)[None, None, :]
    drawn = jnp.where(slot_index == forced_at, S - 2, drawn)
    drawn = jnp.where(slot_index == other_at, 0, drawn)
    return drawn.astype(jnp.int32)


def draw_flexibility(key, part):

    def region_matrix(region_number):
        matrix_key = jax.random.fold_in(jax.random.fold_in(key, 41), region_number)
        first_key, second_key = jax.random.split(matrix_key, 2)
        entries = jax.random.normal(first_key, (M, M), jnp.float32)
        symmetric = (entries + entries.T) * (0.5 / math.sqrt(M))
        diagonal = jax.random.uniform(second_key, (M,), jnp.float32, 1.0, 2.0)
        on_diagonal = jnp.arange(M)[:, None] == jnp.arange(M)[None, :]
        return jnp.where(on_diagonal, diagonal[None, :], symmetric).astype(jnp.bfloat16)
    return lax.map(region_matrix, jnp.arange(REGIONS, dtype=jnp.int32))


def levels(own_key, extent, cuts, smallest, top_value):
    gain = 1.0
    for dim, blocks in cuts:
        draws = jax.random.uniform(jax.random.fold_in(jax.random.fold_in(own_key, 6), dim), (blocks,), jnp.float32, smallest / len(cuts), top_value / len(cuts))
        gain = gain * jnp.repeat(jnp.exp(draws), extent[dim] // blocks).reshape((-1,) + (1,) * (len(extent) - 1 - dim))
    return gain


def bell_draw(rng, dims, spread, reach, shards=(), held_as=jnp.bfloat16):
    gain = levels(rng, dims, shards, -0.22, 0.18) if shards else 1.0
    values = jax.random.normal(rng, dims, jnp.float32) * spread * gain
    return jnp.minimum(jnp.maximum(values, -reach), reach).astype(held_as)


def setup_inputs(seed: int = 0) -> dict:
    keys = jax.random.split(jax.random.key(seed), 8)
    return {
        "multipliers": bell_draw(keys[0], (REGIONS, M, K), 1.0, 6.0, ((0, 16), (1, 2))),
        "flexibility": draw_flexibility(jax.random.fold_in(keys[7], 71), 0),
        "interface_sizes": draw_interface_sizes(jax.random.fold_in(keys[7], 71), 0),
        "send_rows": draw_send_rows(jax.random.fold_in(keys[7], 71), 0),
        "recv_rows": draw_recv_rows(jax.random.fold_in(keys[7], 71), 0),
        "recv_pos": draw_recv_pos(jax.random.fold_in(keys[7], 71), 0),
        "recv_weight": jnp.clip(1.0 * jax.random.uniform(keys[6], (REGIONS, 2, S), jnp.float32) ** levels(keys[6], (REGIONS, 2, S), ((0, 16),), -0.2, 0.2), 0.0, 1.0),
    }


def region_apply(operands):
    matrix, vectors = operands
    return jnp.dot(matrix, vectors, preferred_element_type=jnp.float32)


def pick_rows(settled_region, row_lists):
    return settled_region[row_lists]


def interpolate(arrived, position, weight):
    first_rows = arrived[position].astype(jnp.float32)
    second_rows = arrived[position + 1].astype(jnp.float32)
    return (1.0 - weight)[:, None] * first_rows + weight[:, None] * second_rows


def assemble(settled_region, targets, jumps):
    flat_jumps = jumps.reshape(-1, jumps.shape[-1])
    return settled_region.astype(jnp.float32).at[targets.reshape(-1)].add(-flat_jumps)


def reference(multipliers, flexibility, interface_sizes, send_rows, recv_rows, recv_pos, recv_weight):
    row_ids = jnp.arange(M, dtype=jnp.int32)
    live = (row_ids[None, :] < interface_sizes[:, None])[:, :, None]
    live_multipliers = jnp.where(live, multipliers, jnp.zeros((), multipliers.dtype))
    image = lax.map(region_apply, (flexibility, live_multipliers))
    settled = jnp.where(live, image, jnp.zeros((), image.dtype)).astype(jnp.bfloat16)
    sent = jax.vmap(pick_rows)(settled, send_rows)
    from_lower = jnp.roll(sent[:, 1], 1, axis=0)
    from_upper = jnp.roll(sent[:, 0], -1, axis=0)
    arrived = jnp.stack([from_lower, from_upper], axis=1)
    jumps = jax.vmap(jax.vmap(interpolate))(arrived, recv_pos, recv_weight)
    return jax.vmap(assemble)(settled, recv_rows, jumps)
```

```python
import functools

import jax
import jax.numpy as jnp
from jax import lax
from jax.experimental import pallas as pl
from jax.experimental.pallas import tpu as pltpu
from jax.sharding import PartitionSpec as P

SMEM = pltpu.SMEM


def params():
    return pltpu.CompilerParams(vmem_limit_bytes=56 * 1024 * 1024)


def cost(flops, moved):
    return pl.CostEstimate(flops=flops, bytes_accessed=moved, transcendentals=0)


def tile_of(extent, most):
    tile = most
    while extent % tile:
        tile //= 2
    return tile


def local_kernel(where_ref, flex_ref, other_ref, own_ref, part_ref, near_ref):
    flex = flex_ref[...]
    part_ref[...] = jnp.dot(flex, other_ref[...], preferred_element_type=jnp.float32)
    near_ref[...] = jnp.dot(flex, own_ref[...], preferred_element_type=jnp.float32)


def local_products(where, flex, other, own):
    rows, width = other.shape
    tile = tile_of(rows, 256)
    whole = pl.BlockSpec((rows, width), lambda i, w: (0, 0))
    strip = pl.BlockSpec((tile, width), lambda i, w: (i, 0))
    shape = jax.ShapeDtypeStruct((rows, width), jnp.float32)
    return pl.pallas_call(
        local_kernel,
        out_shape=(shape, shape),
        grid_spec=pltpu.PrefetchScalarGridSpec(
            num_scalar_prefetch=1,
            grid=(rows // tile,),
            in_specs=[pl.BlockSpec((tile, rows), lambda i, w: (i, w[0])), whole, whole],
            out_specs=(strip, strip),
        ),
        compiler_params=params(),
        cost_estimate=cost(4 * rows * rows * width, 2 * rows * rows + 12 * rows * width),
        name="local_products",
    )(where, flex, other, own)


def mirror_kernel(where_ref, flex_ref, own_ref, far_ref):
    far_ref[...] = lax.dot_general(
        flex_ref[...], own_ref[...], (((0,), (0,)), ((), ())),
        preferred_element_type=jnp.float32,
    )


def mirror_product(where, flex, own):
    rows, width = own.shape
    tile = tile_of(rows, 256)
    steps = rows // tile
    return pl.pallas_call(
        mirror_kernel,
        out_shape=jax.ShapeDtypeStruct((rows, width), jnp.float32),
        grid_spec=pltpu.PrefetchScalarGridSpec(
            num_scalar_prefetch=1,
            grid=(steps,),
            in_specs=[
                pl.BlockSpec((rows, tile), lambda i, w: (0, w[1] * steps + i)),
                pl.BlockSpec((rows, width), lambda i, w: (0, 0)),
            ],
            out_specs=pl.BlockSpec((tile, width), lambda i, w: (i, 0)),
        ),
        compiler_params=params(),
        cost_estimate=cost(2 * rows * rows * width, 2 * rows * rows + 6 * rows * width),
        name="mirror_product",
    )(where, flex, own)


def cross_kernel(where_ref, flex_ref, came_ref, near_ref, out_ref):
    out_ref[...] = near_ref[...] + jnp.dot(
        flex_ref[...], came_ref[...], preferred_element_type=jnp.float32
    )


def cross_product(where, flex, came, near):
    rows, width = came.shape
    tile = tile_of(rows, 256)
    strip = pl.BlockSpec((tile, width), lambda i, w: (i, 0))
    return pl.pallas_call(
        cross_kernel,
        out_shape=jax.ShapeDtypeStruct((rows, width), jnp.float32),
        grid_spec=pltpu.PrefetchScalarGridSpec(
            num_scalar_prefetch=1,
            grid=(rows // tile,),
            in_specs=[
                pl.BlockSpec((tile, rows), lambda i, w: (i, w[1])),
                pl.BlockSpec((rows, width), lambda i, w: (0, 0)),
                strip,
            ],
            out_specs=strip,
        ),
        compiler_params=params(),
        cost_estimate=cost(2 * rows * rows * width, 2 * rows * rows + 10 * rows * width),
        name="cross_product",
    )(where, flex, came, near)


def gather_kernel(list_ref, settled_ref, out_ref, rows_ref):
    count = out_ref.shape[0]

    def step(block, carry):
        first = pl.multiple_of(block * 8, 8)
        for k in range(8):
            source = list_ref[first + k]
            rows_ref[pl.ds(first + k, 1), :] = settled_ref[pl.ds(source, 1), :]
        return carry

    lax.fori_loop(0, count // 8, step, 0, unroll=2)
    out_ref[...] = rows_ref[...].astype(out_ref.dtype)


def gather_rows(rows_list, settled):
    count = rows_list.shape[0]
    rows, width = settled.shape
    return pl.pallas_call(
        gather_kernel,
        out_shape=jax.ShapeDtypeStruct((count, width), jnp.bfloat16),
        in_specs=[pl.BlockSpec(memory_space=SMEM), pl.BlockSpec(memory_space=pltpu.VMEM)],
        out_specs=pl.BlockSpec(memory_space=pltpu.VMEM),
        scratch_shapes=[pltpu.VMEM((count, width), jnp.float32)],
        compiler_params=params(),
        cost_estimate=cost(0, 4 * rows * width + 2 * count * width),
        name="gather_rows",
    )(rows_list, settled)


def assemble_kernel(target_ref, pos_ref, weight_ref, base_ref, came_ref, out_ref, rows_ref):
    count = came_ref.shape[0]
    out_ref[...] = base_ref[...]
    rows_ref[...] = came_ref[...].astype(jnp.float32)

    def step(block, carry):
        for k in range(8):
            s = block * 8 + k
            at = pos_ref[s]
            second = weight_ref[s]
            first = 1.0 - second
            jump = first * rows_ref[pl.ds(at, 1), :] + second * rows_ref[pl.ds(at + 1, 1), :]
            row = target_ref[s]
            out_ref[pl.ds(row, 1), :] = out_ref[pl.ds(row, 1), :] - jump
        return carry

    lax.fori_loop(0, count // 8, step, 0)


def assemble(targets, positions, weights, base, came):
    count, width = came.shape
    smem = pl.BlockSpec(memory_space=SMEM)
    vmem = pl.BlockSpec(memory_space=pltpu.VMEM)
    return pl.pallas_call(
        assemble_kernel,
        out_shape=jax.ShapeDtypeStruct(base.shape, jnp.float32),
        in_specs=[smem, smem, smem, vmem, vmem],
        out_specs=vmem,
        scratch_shapes=[pltpu.VMEM((count, width), jnp.float32)],
        compiler_params=params(),
        cost_estimate=cost(0, 8 * base.size + 2 * came.size),
        name="assemble",
    )(targets, positions, weights, base, came)


def on_device(
    multipliers, flexibility, interface_sizes, send_rows, recv_rows, recv_pos, recv_weight
):
    block = multipliers[0]
    flex = flexibility[0]
    rows, cases = block.shape
    width = cases // 2
    me = lax.axis_index("panel")
    other = 1 - me
    region = lax.axis_index("region")
    regions = lax.axis_size("region")
    side = region % 2
    size = interface_sizes[0]
    swap = [(0, 1), (1, 0)]
    inner = [(r, r ^ 1) for r in range(regions)]
    outer = [(r, (r + (1 if r % 2 else -1)) % regions) for r in range(regions)]

    ids = jnp.arange(rows, dtype=jnp.int32)[:, None]
    live_here = me * rows + ids < size
    live_there = other * rows + ids < size
    live_block = jnp.where(live_here, block, jnp.zeros((), block.dtype))
    own = lax.dynamic_slice_in_dim(live_block, me * width, width, axis=1)
    others = lax.dynamic_slice_in_dim(live_block, other * width, width, axis=1)
    came = lax.ppermute(others, "panel", swap)

    where = jnp.stack([me, other]).astype(jnp.int32)
    part, near = local_products(where, flex, others, own)
    top = jnp.maximum(jnp.max(jnp.abs(part)), 1e-30)
    power = jnp.floor(jnp.log2(top)) - 13.0
    payload = jnp.concatenate(
        [
            (part * jnp.exp2(-power)).astype(jnp.float16),
            jnp.full((16, width), power, jnp.float16),
        ],
        axis=0,
    )
    payload = lax.ppermute(payload, "panel", swap)
    far = mirror_product(where, flex, own)
    image_here = cross_product(where, flex, came, near)

    came_part = payload[:rows].astype(jnp.float32)
    came_power = jnp.exp2(payload[rows, 0].astype(jnp.float32))
    image_there = far + came_part * came_power
    zero = jnp.zeros((), jnp.float32)
    here = jnp.where(live_here, image_here, zero)
    there = jnp.where(live_there, image_there, zero)
    first = jnp.where(me == 0, here, there)
    last = jnp.where(me == 0, there, here)
    settled = lax.reduce_precision(jnp.concatenate([first, last], axis=0), 8, 7)

    lists = send_rows[region]
    slow = gather_rows(lists[side], settled)
    slow = lax.ppermute(slow, "region", outer)
    fast = gather_rows(lists[1 - side], settled)
    fast = lax.ppermute(fast, "region", inner)
    up = 1 - side
    result = assemble(recv_rows[0, up], recv_pos[0, up], recv_weight[0, up], settled, fast)
    result = assemble(recv_rows[0, side], recv_pos[0, side], recv_weight[0, side], result, slow)
    return result[None]


def solution(mesh):
    assert mesh.shape["panel"] == 2 and mesh.shape["region"] % 2 == 0
    in_specs = (
        P("region", "panel", None),
        P("region", "panel", None),
        P("region"),
        P(),
        P("region", None, None),
        P("region", None, None),
        P("region", None, None),
    )
    out_specs = P("region", None, "panel")
    return jax.shard_map(
        on_device, mesh=mesh, in_specs=in_specs, out_specs=out_specs, check_vma=False
    )
```

```python
import jax
import jax.numpy as jnp
from jax import lax
from jax.experimental import pallas as pl
from jax.experimental.pallas import tpu as pltpu
from jax.sharding import PartitionSpec as P

SMEM = pl.BlockSpec(memory_space=pltpu.SMEM)
VMEM = pl.BlockSpec(memory_space=pltpu.VMEM)
ANY = pl.BlockSpec(memory_space=pl.ANY)
HBM = pl.BlockSpec(memory_space=pltpu.HBM)
LANES = 128
F32 = jnp.float32
BF16 = jnp.bfloat16


def params(mebibytes):
    return pltpu.CompilerParams(vmem_limit_bytes=mebibytes * 1024 * 1024)


def cost(flops, moved):
    return pl.CostEstimate(flops=flops, bytes_accessed=moved, transcendentals=0)


def tile_of(extent, most):
    tile = most
    while extent % tile:
        tile //= 2
    return tile


def strips_of(flex_ref, block, buffer_ref, sems):
    rows = buffer_ref.shape[0]
    count = sems.shape[0]
    tile = rows // count
    start = pl.multiple_of(block * rows, rows)
    copies = []
    for i in range(count):
        span = pl.ds(i * tile, tile)
        copy = pltpu.make_async_copy(
            flex_ref.at[span, pl.ds(start, rows)], buffer_ref.at[span, :], sems.at[i]
        )
        copy.start()
        copies.append(copy)
    return copies, tile


def store_chunks(refs, span, value):
    for c, ref in enumerate(refs):
        ref[span, :] = value[:, c * LANES : (c + 1) * LANES]


def masked(ref, live):
    value = ref[...]
    ids = lax.broadcasted_iota(jnp.int32, value.shape, 0)
    return jnp.where(ids < live, value, jnp.zeros_like(value))


def part_kernel(where_ref, flex_ref, other_ref, *rest):
    outs, buffer_ref, sems = rest[:-2], rest[-2], rest[-1]
    copies, tile = strips_of(flex_ref, where_ref[0], buffer_ref, sems)
    right = masked(other_ref, where_ref[2])
    rows = buffer_ref.shape[0]
    most = jnp.zeros((8, right.shape[1]), F32)
    for i, copy in enumerate(copies):
        copy.wait()
        span = pl.ds(i * tile, tile)
        part = jnp.dot(buffer_ref[span, :], right, preferred_element_type=F32)
        store_chunks(outs, span, part)
        most = jnp.maximum(most, jnp.max(jnp.abs(part).reshape(-1, 8, part.shape[1]), axis=0))
    top = jnp.maximum(jnp.max(most, keepdims=True), 1e-30)
    power = jnp.floor(jnp.log2(top)) - 13.0
    scale = jnp.exp2(-power)
    for ref in outs:
        ref[pl.ds(0, rows), :] = ref[pl.ds(0, rows), :] * scale
        ref[pl.ds(rows, 16), :] = jnp.broadcast_to(power, (16, LANES))


def cross_kernel(where_ref, flex_ref, came_ref, *rest):
    count = (len(rest) - 2) // 2
    nears, outs, buffer_ref, sems = rest[:count], rest[count:-2], rest[-2], rest[-1]
    copies, tile = strips_of(flex_ref, where_ref[1], buffer_ref, sems)
    right = masked(came_ref, where_ref[3])
    for i, copy in enumerate(copies):
        copy.wait()
        span = pl.ds(i * tile, tile)
        image = jnp.dot(buffer_ref[span, :], right, preferred_element_type=F32)
        image = image + jnp.concatenate([ref[span, :] for ref in nears], axis=1)
        ids = i * tile + lax.broadcasted_iota(jnp.int32, image.shape, 0)
        image = jnp.where(ids < where_ref[2], image, jnp.zeros_like(image))
        store_chunks(outs, span, image.astype(BF16).astype(F32))


def product(kernel, name, out_shapes, where, flex, *rights):
    rows = flex.shape[0]
    width = rights[0].shape[1]
    strips = rows // tile_of(rows, 512)
    return pl.pallas_call(
        kernel,
        out_shape=tuple(jax.ShapeDtypeStruct(shape, F32) for shape in out_shapes),
        in_specs=[SMEM, HBM] + [VMEM] * len(rights),
        out_specs=tuple(VMEM for _ in out_shapes),
        scratch_shapes=[
            pltpu.VMEM((rows, rows), BF16),
            pltpu.SemaphoreType.DMA((strips,)),
        ],
        compiler_params=params(50),
        cost_estimate=cost(2 * rows * rows * width, 2 * rows * rows + 6 * rows * width),
        name=name,
    )(where, flex, *rights)


def own_kernel(where_ref, flex_ref, own_ref, *outs):
    tile = flex_ref.shape[0]
    rows = own_ref.shape[0]
    chunks = len(outs) // 2
    step = pl.program_id(0)
    right = masked(own_ref, where_ref[2])
    columns = [pl.ds(pl.multiple_of(where_ref[b] * rows, rows), rows) for b in range(2)]
    near = jnp.dot(flex_ref[:, columns[0]], right, preferred_element_type=F32)
    store_chunks(outs[:chunks], slice(None), near)
    span = pl.ds(pl.multiple_of(step * tile, tile), tile)
    mine = own_ref[span, :]
    ids = step * tile + lax.broadcasted_iota(jnp.int32, mine.shape, 0)
    mine = jnp.where(ids < where_ref[2], mine, jnp.zeros_like(mine))
    far = lax.dot_general(
        flex_ref[:, columns[1]], mine, (((0,), (0,)), ((), ())), preferred_element_type=F32
    )
    for c, ref in enumerate(outs[chunks:]):
        piece = far[:, c * LANES : (c + 1) * LANES]

        @pl.when(step == 0)
        def _():
            ref[...] = piece

        @pl.when(step > 0)
        def _():
            ref[...] = ref[...] + piece


def own_products(where, flex, own):
    rows, width = own.shape
    chunks = width // LANES
    tile = tile_of(rows, 512)
    shape = jax.ShapeDtypeStruct((rows, LANES), F32)
    outs = pl.pallas_call(
        own_kernel,
        out_shape=(shape,) * (2 * chunks),
        grid_spec=pltpu.PrefetchScalarGridSpec(
            num_scalar_prefetch=1,
            grid=(rows // tile,),
            in_specs=[
                pl.BlockSpec((tile, 2 * rows), lambda i, w: (i, 0)),
                pl.BlockSpec((rows, width), lambda i, w: (0, 0)),
            ],
            out_specs=(pl.BlockSpec((tile, LANES), lambda i, w: (i, 0)),) * chunks
            + (pl.BlockSpec((rows, LANES), lambda i, w: (0, 0)),) * chunks,
        ),
        compiler_params=params(50),
        cost_estimate=cost(4 * rows * rows * width, 4 * rows * rows + 10 * rows * width),
        name="own_products",
    )(where, flex, own)
    return outs[:chunks], outs[chunks:]


def pick_rows(list_ref, settled_ref, out_ref, rows_ref):
    count = out_ref.shape[0]
    group = tile_of(count, 32)

    def step(block, carry):
        first = pl.multiple_of(block * group, group)
        for k in range(group):
            source = list_ref[first + k]
            rows_ref[pl.ds(first + k, 1), :] = settled_ref[pl.ds(source, 1), :]
        return carry

    lax.fori_loop(0, count // group, step, 0)
    out_ref[...] = rows_ref[...].astype(out_ref.dtype)


def settle_kernel(list_ref, live_ref, here_ref, far_ref, came_ref, settled_ref, out_ref, rows_ref):
    rows = far_ref.shape[0]
    settled_ref[pl.ds(0, rows), :] = here_ref[...]
    grown = jnp.exp2(came_ref[pl.ds(rows, 1), :])
    there = far_ref[...] + came_ref[pl.ds(0, rows), :] * grown
    ids = lax.broadcasted_iota(jnp.int32, there.shape, 0)
    there = jnp.where(ids < live_ref[0], there, jnp.zeros_like(there))
    settled_ref[pl.ds(rows, rows), :] = there.astype(BF16).astype(F32)
    pick_rows(list_ref, settled_ref, out_ref, rows_ref)


def settle(rows_list, live, here, far, came):
    count = rows_list.shape[0]
    rows, lanes = far.shape
    return pl.pallas_call(
        settle_kernel,
        out_shape=(
            jax.ShapeDtypeStruct((2 * rows, lanes), F32),
            jax.ShapeDtypeStruct((count, lanes), BF16),
        ),
        in_specs=[SMEM, SMEM, VMEM, VMEM, VMEM],
        out_specs=(VMEM, VMEM),
        scratch_shapes=[pltpu.VMEM((count, lanes), F32)],
        compiler_params=params(20),
        cost_estimate=cost(0, 20 * rows * lanes + 2 * count * lanes),
        name="settle",
    )(rows_list, live, here, far, came)


def gather_rows(rows_list, settled):
    count = rows_list.shape[0]
    lanes = settled.shape[1]
    return pl.pallas_call(
        pick_rows,
        out_shape=jax.ShapeDtypeStruct((count, lanes), BF16),
        in_specs=[SMEM, VMEM],
        out_specs=VMEM,
        scratch_shapes=[pltpu.VMEM((count, lanes), F32)],
        compiler_params=params(8),
        cost_estimate=cost(0, 4 * settled.size + 2 * count * lanes),
        name="gather_rows",
    )(rows_list, settled)


def assemble_kernel(
    chunk, blocks_ref, targets_ref, places_ref, weights_ref, settled_ref, fast_ref, slow_ref, *rest
):
    out_ref, rows_refs, sums, sems = rest[-8], rest[-7:-5], rest[-5:-1], rest[-1]
    rows_refs[0][...] = fast_ref[...].astype(F32)
    rows_refs[1][...] = slow_ref[...].astype(F32)
    for ref in sums:
        ref[...] = jnp.zeros_like(ref)
    count = fast_ref.shape[0]
    group = tile_of(count, 32)

    def step(block, carry):
        start = pl.multiple_of(block * group, group)
        for k in range(group):
            for j in range(2):
                s = j * count + start + k
                row = targets_ref[s]
                at = places_ref[s]
                weight = weights_ref[pl.ds(s, 1), :]
                first = rows_refs[j][pl.ds(at, 1), :]
                second = rows_refs[j][pl.ds(at + 1, 1), :]
                jump = (1.0 - weight) * first + weight * second
                total = sums[(k % 2) * 2 + j]
                total[pl.ds(row, 1), :] = total[pl.ds(row, 1), :] + jump
        return carry

    lax.fori_loop(0, count // group, step, 0)
    rows = settled_ref.shape[0]
    piece = rows // 4
    copies = []
    for q in range(4):
        span = pl.ds(q * piece, piece)
        sums[0][span, :] = settled_ref[span, :] - (
            (sums[0][span, :] + sums[1][span, :]) + (sums[2][span, :] + sums[3][span, :])
        )
        target = pl.multiple_of(blocks_ref[q // 2] * (rows // 2) + (q % 2) * piece, piece)
        copy = pltpu.make_async_copy(
            sums[0].at[span, :],
            out_ref.at[pl.ds(target, piece), pl.ds(chunk * LANES, LANES)],
            sems.at[q],
        )
        copy.start()
        copies.append(copy)
    for copy in copies:
        copy.wait()


def assemble(chunk, width, blocks, targets, places, weights, settled, fast, slow, before):
    rows = settled.shape[0]
    count = fast.shape[0]
    more = [] if before is None else [before]
    return pl.pallas_call(
        lambda *refs: assemble_kernel(chunk, *refs),
        out_shape=jax.ShapeDtypeStruct((rows, width), F32),
        in_specs=[SMEM, SMEM, SMEM, VMEM, VMEM, VMEM, VMEM] + [ANY] * len(more),
        out_specs=ANY,
        scratch_shapes=[pltpu.VMEM((count, LANES), F32)] * 2
        + [pltpu.VMEM((rows, LANES), F32)] * 4
        + [pltpu.SemaphoreType.DMA((4,))],
        input_output_aliases={7: 0} if more else {},
        compiler_params=params(20),
        cost_estimate=cost(0, 8 * settled.size + 4 * fast.size),
        name="assemble",
    )(blocks, targets, places, weights, settled, fast, slow, *more)


def after(value, *earlier):
    return lax.optimization_barrier((value, *earlier))[0]


def on_device(
    multipliers, flexibility, interface_sizes, send_rows, recv_rows, recv_pos, recv_weight
):
    block = multipliers[0]
    flex = flexibility[0]
    rows, cases = block.shape
    width = cases // 2
    chunks = width // LANES
    me = lax.axis_index("panel")
    other = 1 - me
    region = lax.axis_index("region")
    regions = lax.axis_size("region")
    side = region % 2
    size = interface_sizes[0]
    swap = [(0, 1), (1, 0)]
    inner = [(r, r ^ 1) for r in range(regions)]
    outer = [(r, (r + (1 if r % 2 else -1)) % regions) for r in range(regions)]

    live_here = size - me * rows
    live_there = size - other * rows
    where = jnp.stack([me, other, live_here, live_there]).astype(jnp.int32)
    others = lax.dynamic_slice_in_dim(block, other * width, width, axis=1)
    came = lax.ppermute(others, "panel", swap)
    strip = (rows, LANES)

    def local_order(index):
        return (index + me * rows) % (2 * rows)

    lists = local_order(send_rows[region])
    slow_list, fast_list = lists[side], lists[1 - side]

    def ordered(table):
        return jnp.where(side == 0, table[::-1], table).reshape(-1)

    targets = ordered(local_order(recv_rows[0]))
    places = ordered(recv_pos[0])
    weights = jnp.broadcast_to(ordered(recv_weight[0])[:, None], (targets.shape[0], LANES))
    blocks = where[:2]
    live = live_there[None]

    parts = product(
        part_kernel, "part_product", [(rows + 16, LANES)] * chunks, where, flex, others
    )
    payloads = []
    order = others
    for c in range(chunks):
        order = after(parts[c], order).astype(jnp.float16)
        payloads.append(lax.ppermute(order, "panel", swap))
    own = lax.dynamic_slice_in_dim(after(block, order), me * width, width, axis=1)
    own, targets, places, weights, slow_list, fast_list = lax.optimization_barrier(
        (own, targets, places, weights, slow_list, fast_list)
    )
    nears, fars = own_products(where, flex, own)
    heres = product(
        cross_kernel, "cross_product", [strip] * chunks, where, flex, came, *nears
    )

    settled, slow, fast = [], [], []
    last = heres[0]
    for c in range(chunks):
        arrived = after(payloads[c], last).astype(F32)
        whole, sent = settle(slow_list, live, heres[c], fars[c], arrived)
        settled.append(whole)
        slow.append(lax.ppermute(sent, "region", outer))
        last = gather_rows(after(fast_list, sent), whole)
        fast.append(lax.ppermute(last, "region", inner))
    targets = after(targets, last)
    result = None
    for c in range(chunks):
        result = assemble(
            c, width, blocks, targets, places, weights, settled[c], fast[c], slow[c], result
        )
    return result[None]


def solution(mesh):
    assert mesh.shape["panel"] == 2 and mesh.shape["region"] % 2 == 0
    in_specs = (
        P("region", "panel", None),
        P("region", "panel", None),
        P("region"),
        P(),
        P("region", None, None),
        P("region", None, None),
        P("region", None, None),
    )
    out_specs = P("region", None, "panel")
    return jax.shard_map(
        on_device, mesh=mesh, in_specs=in_specs, out_specs=out_specs, check_vma=False
    )
```

```python
import jax
import jax.numpy as jnp
from jax import lax
from jax.experimental import pallas as pl
from jax.experimental.pallas import tpu as pltpu
from jax.sharding import PartitionSpec as P


SMEM = pl.BlockSpec(memory_space=pltpu.SMEM)
VMEM = pl.BlockSpec(memory_space=pltpu.VMEM)
ANY = pl.BlockSpec(memory_space=pl.ANY)
HBM = pl.BlockSpec(memory_space=pltpu.HBM)
LANES = 128
LIMIT = 50
F32 = jnp.float32
BF16 = jnp.bfloat16


def params(mebibytes):
    return pltpu.CompilerParams(vmem_limit_bytes=mebibytes * 1024 * 1024)


def cost(flops, moved):
    return pl.CostEstimate(flops=flops, bytes_accessed=moved, transcendentals=0)


def tile_of(extent, most):
    tile = most
    while extent % tile:
        tile //= 2
    return tile


def strips_of(flex_ref, block, buffer_ref, sems):
    rows = buffer_ref.shape[0]
    count = sems.shape[0]
    tile = rows // count
    start = pl.multiple_of(block * rows, rows)
    copies = []
    for i in range(count):
        span = pl.ds(i * tile, tile)
        copy = pltpu.make_async_copy(
            flex_ref.at[span, pl.ds(start, rows)], buffer_ref.at[span, :], sems.at[i]
        )
        copy.start()
        copies.append(copy)
    return copies, tile


def store_chunks(refs, span, value):
    for c, ref in enumerate(refs):
        ref[span, :] = value[:, c * LANES : (c + 1) * LANES]


def masked(ref, live):
    value = ref[...]
    ids = lax.broadcasted_iota(jnp.int32, value.shape, 0)
    return jnp.where(ids < live, value, jnp.zeros_like(value))


def part_kernel(where_ref, flex_ref, other_ref, *rest):
    outs, buffer_ref, sems = rest[:-2], rest[-2], rest[-1]
    copies, tile = strips_of(flex_ref, where_ref[0], buffer_ref, sems)
    right = masked(other_ref, where_ref[2])
    rows = buffer_ref.shape[0]
    most = jnp.zeros((8, right.shape[1]), F32)
    for i, copy in enumerate(copies):
        copy.wait()
        span = pl.ds(i * tile, tile)
        part = jnp.dot(buffer_ref[span, :], right, preferred_element_type=F32)
        store_chunks(outs, span, part)
        most = jnp.maximum(most, jnp.max(jnp.abs(part).reshape(-1, 8, part.shape[1]), axis=0))
    top = jnp.maximum(jnp.max(most, keepdims=True), 1e-30)
    power = jnp.floor(jnp.log2(top)) - 13.0
    scale = jnp.exp2(-power)
    for ref in outs:
        ref[pl.ds(0, rows), :] = ref[pl.ds(0, rows), :] * scale
        ref[pl.ds(rows, 16), :] = jnp.broadcast_to(power, (16, LANES))


def product(kernel, out_shapes, where, flex, *rights):
    rows = flex.shape[0]
    width = rights[0].shape[1]
    strips = rows // tile_of(rows, 512)
    return pl.pallas_call(
        kernel,
        out_shape=tuple(jax.ShapeDtypeStruct(shape, F32) for shape in out_shapes),
        in_specs=[SMEM, HBM] + [VMEM] * len(rights),
        out_specs=tuple(VMEM for _ in out_shapes),
        scratch_shapes=[
            pltpu.VMEM((rows, rows), BF16),
            pltpu.SemaphoreType.DMA((strips,)),
        ],
        compiler_params=params(LIMIT),
        cost_estimate=cost(2 * rows * rows * width, 2 * rows * rows + 6 * rows * width),
    )(where, flex, *rights)


def mirror_kernel(where_ref, flex_ref, own_ref, *outs):
    right = masked(own_ref, where_ref[2])
    far = lax.dot_general(
        flex_ref[...], right, (((0,), (0,)), ((), ())), preferred_element_type=F32
    )
    store_chunks(outs, slice(None), far)


def mirror_product(where, flex, own):
    rows, width = own.shape
    chunks = width // LANES
    tile = tile_of(rows, 1024)
    steps = rows // tile
    return pl.pallas_call(
        mirror_kernel,
        out_shape=(jax.ShapeDtypeStruct((rows, LANES), F32),) * chunks,
        grid_spec=pltpu.PrefetchScalarGridSpec(
            num_scalar_prefetch=1,
            grid=(steps,),
            in_specs=[
                pl.BlockSpec((rows, tile), lambda i, w: (0, w[1] * steps + i)),
                pl.BlockSpec((rows, width), lambda i, w: (0, 0)),
            ],
            out_specs=(pl.BlockSpec((tile, LANES), lambda i, w: (i, 0)),) * chunks,
        ),
        compiler_params=params(LIMIT),
        cost_estimate=cost(2 * rows * rows * width, 2 * rows * rows + 6 * rows * width),
        name="mirror_product",
    )(where, flex, own)


def image_kernel(where_ref, flex_ref, own_ref, came_ref, *rest):
    outs, whole_ref = rest[:-1], rest[-1]
    rows = own_ref.shape[0]
    tile = flex_ref.shape[0]
    step = pl.program_id(0)

    @pl.when(step == 0)
    def _():
        for j, ref in enumerate((own_ref, came_ref)):
            span = pl.ds(pl.multiple_of(where_ref[j] * rows, rows), rows)
            whole_ref[span, :] = masked(ref, where_ref[2 + j])

    image = jnp.dot(flex_ref[...], whole_ref[...], preferred_element_type=F32)
    ids = step * tile + lax.broadcasted_iota(jnp.int32, image.shape, 0)
    image = jnp.where(ids < where_ref[2], image, jnp.zeros_like(image))
    store_chunks(outs, slice(None), image.astype(BF16).astype(F32))


def image_product(where, flex, own, came):
    rows, width = own.shape
    chunks = width // LANES
    tile = tile_of(rows, 512)
    whole = pl.BlockSpec((rows, width), lambda i, w: (0, 0))
    return pl.pallas_call(
        image_kernel,
        out_shape=(jax.ShapeDtypeStruct((rows, LANES), F32),) * chunks,
        grid_spec=pltpu.PrefetchScalarGridSpec(
            num_scalar_prefetch=1,
            grid=(rows // tile,),
            in_specs=[pl.BlockSpec((tile, 2 * rows), lambda i, w: (i, 0)), whole, whole],
            out_specs=(pl.BlockSpec((tile, LANES), lambda i, w: (i, 0)),) * chunks,
            scratch_shapes=[pltpu.VMEM((2 * rows, width), BF16)],
        ),
        compiler_params=params(LIMIT),
        cost_estimate=cost(4 * rows * rows * width, 4 * rows * rows + 6 * rows * width),
        name="image_product",
    )(where, flex, own, came)


def pick_rows(list_ref, settled_ref, out_ref, rows_ref):
    count = out_ref.shape[0]
    group = tile_of(count, 128)

    def step(block, carry):
        first = pl.multiple_of(block * group, group)
        for k in range(group):
            source = list_ref[first + k]
            rows_ref[pl.ds(first + k, 1), :] = settled_ref[pl.ds(source, 1), :]
        return carry

    lax.fori_loop(0, count // group, step, 0)
    out_ref[...] = rows_ref[...].astype(out_ref.dtype)


def settle_kernel(list_ref, live_ref, here_ref, far_ref, came_ref, settled_ref, out_ref, rows_ref):
    rows = far_ref.shape[0]
    settled_ref[pl.ds(0, rows), :] = here_ref[...]
    grown = jnp.exp2(came_ref[pl.ds(rows, 1), :])
    there = far_ref[...] + came_ref[pl.ds(0, rows), :] * grown
    ids = lax.broadcasted_iota(jnp.int32, there.shape, 0)
    there = jnp.where(ids < live_ref[0], there, jnp.zeros_like(there))
    settled_ref[pl.ds(rows, rows), :] = there.astype(BF16).astype(F32)
    pick_rows(list_ref, settled_ref, out_ref, rows_ref)


def settle(rows_list, live, here, far, came):
    count = rows_list.shape[0]
    rows, lanes = far.shape
    return pl.pallas_call(
        settle_kernel,
        out_shape=(
            jax.ShapeDtypeStruct((2 * rows, lanes), F32),
            jax.ShapeDtypeStruct((count, lanes), BF16),
        ),
        in_specs=[SMEM, SMEM, VMEM, VMEM, VMEM],
        out_specs=(VMEM, VMEM),
        scratch_shapes=[pltpu.VMEM((count, lanes), F32)],
        compiler_params=params(20),
        cost_estimate=cost(0, 20 * rows * lanes + 2 * count * lanes),
        name="settle",
    )(rows_list, live, here, far, came)


def gather_rows(rows_list, settled):
    count = rows_list.shape[0]
    lanes = settled.shape[1]
    return pl.pallas_call(
        pick_rows,
        out_shape=jax.ShapeDtypeStruct((count, lanes), BF16),
        in_specs=[SMEM, VMEM],
        out_specs=VMEM,
        scratch_shapes=[pltpu.VMEM((count, lanes), F32)],
        compiler_params=params(8),
        cost_estimate=cost(0, 4 * settled.size + 2 * count * lanes),
        name="gather_rows",
    )(rows_list, settled)


def assemble_kernel(chunk, blocks_ref, *refs):
    tables = (refs[0:3], refs[3:6])
    settled_ref, cames = refs[6], refs[7:9]
    out_ref, rows_refs, sums, sems = refs[-8], refs[-7:-5], refs[-5:-1], refs[-1]
    for j in range(2):
        rows_refs[j][...] = cames[j][...].astype(F32)
        sums[2 * j + 1][...] = jnp.zeros_like(settled_ref)
    sums[0][...] = settled_ref[...]
    sums[2][...] = jnp.zeros_like(settled_ref)
    count = cames[0].shape[0]
    group = tile_of(count, 64)

    def step(block, carry):
        start = pl.multiple_of(block * group, group)
        for k in range(group):
            s = start + k
            for j in range(2):
                targets_ref, places_ref, weights_ref = tables[j]
                row = targets_ref[s]
                at = places_ref[s]
                weight = weights_ref[pl.ds(s, 1), :]
                first = rows_refs[j][pl.ds(at, 1), :]
                second = rows_refs[j][pl.ds(at + 1, 1), :]
                jump = (1.0 - weight) * first + weight * second
                total = sums[2 * (k % 2) + j]
                total[pl.ds(row, 1), :] = total[pl.ds(row, 1), :] - jump
        return carry

    lax.fori_loop(0, count // group, step, 0)
    rows = settled_ref.shape[0]
    piece = rows // 8
    copies = []
    for q in range(8):
        span = pl.ds(q * piece, piece)
        sums[0][span, :] = (sums[0][span, :] + sums[1][span, :]) + (
            sums[2][span, :] + sums[3][span, :]
        )
        target = pl.multiple_of(blocks_ref[q // 4] * (rows // 2) + (q % 4) * piece, piece)
        copy = pltpu.make_async_copy(
            sums[0].at[span, :],
            out_ref.at[pl.ds(target, piece), pl.ds(chunk * LANES, LANES)],
            sems.at[q],
        )
        copy.start()
        copies.append(copy)
    for copy in copies:
        copy.wait()


def assemble(chunk, width, blocks, tables, settled, fast, slow, before):
    rows = settled.shape[0]
    count = fast.shape[0]
    more = [] if before is None else [before]
    return pl.pallas_call(
        lambda *refs: assemble_kernel(chunk, *refs),
        out_shape=jax.ShapeDtypeStruct((rows, width), F32),
        in_specs=[SMEM] + [SMEM, SMEM, VMEM] * 2 + [VMEM] * 3 + [ANY] * len(more),
        out_specs=ANY,
        scratch_shapes=[pltpu.VMEM((count, LANES), F32)] * 2
        + [pltpu.VMEM((rows, LANES), F32)] * 4
        + [pltpu.SemaphoreType.DMA((8,))],
        input_output_aliases={10: 0} if more else {},
        compiler_params=params(20),
        cost_estimate=cost(0, 8 * settled.size + 4 * fast.size),
        name="assemble",
    )(blocks, *tables[0], *tables[1], settled, fast, slow, *more)


def after(value, *earlier):
    return lax.optimization_barrier((value, *earlier))[0]


def on_device(
    multipliers, flexibility, interface_sizes, send_rows, recv_rows, recv_pos, recv_weight
):
    block = multipliers[0]
    flex = flexibility[0]
    rows, cases = block.shape
    width = cases // 2
    chunks = width // LANES
    me = lax.axis_index("panel")
    other = 1 - me
    region = lax.axis_index("region")
    regions = lax.axis_size("region")
    side = region % 2
    size = interface_sizes[0]
    swap = [(0, 1), (1, 0)]
    inner = [(r, r ^ 1) for r in range(regions)]
    outer = [(r, (r + (1 if r % 2 else -1)) % regions) for r in range(regions)]

    live_here = size - me * rows
    live_there = size - other * rows
    where = jnp.stack([me, other, live_here, live_there]).astype(jnp.int32)
    others = lax.dynamic_slice_in_dim(block, other * width, width, axis=1)
    came = lax.ppermute(others, "panel", swap)

    def local_order(index):
        return (index + me * rows) % (2 * rows)

    lists = local_order(send_rows[region])
    slow_list, fast_list = lists[side], lists[1 - side]

    recv_local = local_order(recv_rows[0])
    tables = []
    for j in (1 - side, side):
        weight = jnp.broadcast_to(recv_weight[0][j][:, None], (recv_rows.shape[2], LANES))
        tables.append((recv_local[j], recv_pos[0][j], weight))
    blocks = where[:2]
    live = live_there[None]

    own = lax.dynamic_slice_in_dim(after(block, others), me * width, width, axis=1)
    own, tables, slow_list, fast_list, blocks, live, held = lax.optimization_barrier(
        (own, tables, slow_list, fast_list, blocks, live, others)
    )
    parts = product(part_kernel, [(rows + 16, LANES)] * chunks, where, flex, held)
    payloads = []
    order = others
    for c in range(chunks):
        order = after(parts[c], order).astype(jnp.float16)
        payloads.append(lax.ppermute(order, "panel", swap))
    fars = mirror_product(where, flex, after(own, order))
    own = after(own, fars)
    heres = image_product(where, flex, own, came)

    settled, slow, fast = [], [], []
    last = heres[0]
    for c in range(chunks):
        arrived = after(payloads[c], last).astype(F32)
        whole, sent = settle(slow_list, live, heres[c], fars[c], arrived)
        slow.append(lax.ppermute(sent, "region", outer))
        last = gather_rows(after(fast_list, sent), whole)
        fast.append(lax.ppermute(last, "region", inner))
        settled.append(whole)
    blocks = after(blocks, last)
    result = None
    for c in range(chunks):
        result = assemble(c, width, blocks, tables, settled[c], fast[c], slow[c], result)
    return result[None]


def solution(mesh):
    assert mesh.shape["panel"] == 2 and mesh.shape["region"] % 2 == 0
    in_specs = (
        P("region", "panel", None),
        P("region", "panel", None),
        P("region"),
        P(),
        P("region", None, None),
        P("region", None, None),
        P("region", None, None),
    )
    out_specs = P("region", None, "panel")
    return jax.shard_map(
        on_device, mesh=mesh, in_specs=in_specs, out_specs=out_specs, check_vma=False
    )
```

```python
import jax
import jax.numpy as jnp
from jax import lax
from jax.experimental import pallas as pl
from jax.experimental.pallas import tpu as pltpu
from jax.sharding import PartitionSpec as P


SMEM = pl.BlockSpec(memory_space=pltpu.SMEM)
VMEM = pl.BlockSpec(memory_space=pltpu.VMEM)
ANY = pl.BlockSpec(memory_space=pl.ANY)
HBM = pl.BlockSpec(memory_space=pltpu.HBM)
LANES = 128
LIMIT = 50
F32 = jnp.float32
BF16 = jnp.bfloat16


def params(mebibytes):
    return pltpu.CompilerParams(vmem_limit_bytes=mebibytes * 1024 * 1024)


def cost(flops, moved):
    return pl.CostEstimate(flops=flops, bytes_accessed=moved, transcendentals=0)


def tile_of(extent, most):
    tile = most
    while extent % tile:
        tile //= 2
    return tile


def strips_of(flex_ref, block, buffer_ref, sems):
    rows = buffer_ref.shape[0]
    count = sems.shape[0]
    tile = rows // count
    start = pl.multiple_of(block * rows, rows)
    copies = []
    for i in range(count):
        span = pl.ds(i * tile, tile)
        copy = pltpu.make_async_copy(
            flex_ref.at[span, pl.ds(start, rows)], buffer_ref.at[span, :], sems.at[i]
        )
        copy.start()
        copies.append(copy)
    return copies, tile


def store_chunks(refs, span, value):
    for c, ref in enumerate(refs):
        ref[span, :] = value[:, c * LANES : (c + 1) * LANES]


def masked(ref, live):
    value = ref[...]
    ids = lax.broadcasted_iota(jnp.int32, value.shape, 0)
    return jnp.where(ids < live, value, jnp.zeros_like(value))


def part_kernel(where_ref, flex_ref, other_ref, *rest):
    outs, buffer_ref, sems = rest[:-2], rest[-2], rest[-1]
    copies, tile = strips_of(flex_ref, where_ref[0], buffer_ref, sems)
    right = masked(other_ref, where_ref[2])
    rows = buffer_ref.shape[0]
    most = jnp.zeros((8, right.shape[1]), F32)
    for i, copy in enumerate(copies):
        copy.wait()
        span = pl.ds(i * tile, tile)
        part = jnp.dot(buffer_ref[span, :], right, preferred_element_type=F32)
        store_chunks(outs, span, part)
        most = jnp.maximum(most, jnp.max(jnp.abs(part).reshape(-1, 8, part.shape[1]), axis=0))
    top = jnp.maximum(jnp.max(most, keepdims=True), 1e-30)
    power = jnp.floor(jnp.log2(top)) - 13.0
    scale = jnp.exp2(-power)
    for ref in outs:
        ref[pl.ds(0, rows), :] = ref[pl.ds(0, rows), :] * scale
        ref[pl.ds(rows, 16), :] = jnp.broadcast_to(power, (16, LANES))


def product(kernel, out_shapes, where, flex, *rights):
    rows = flex.shape[0]
    width = rights[0].shape[1]
    strips = rows // tile_of(rows, 512)
    return pl.pallas_call(
        kernel,
        out_shape=tuple(jax.ShapeDtypeStruct(shape, F32) for shape in out_shapes),
        in_specs=[SMEM, HBM] + [VMEM] * len(rights),
        out_specs=tuple(VMEM for _ in out_shapes),
        scratch_shapes=[
            pltpu.VMEM((rows, rows), BF16),
            pltpu.SemaphoreType.DMA((strips,)),
        ],
        compiler_params=params(LIMIT),
        cost_estimate=cost(2 * rows * rows * width, 2 * rows * rows + 6 * rows * width),
    )(where, flex, *rights)


def mirror_kernel(where_ref, flex_ref, own_ref, *outs):
    right = masked(own_ref, where_ref[2])
    far = lax.dot_general(
        flex_ref[...], right, (((0,), (0,)), ((), ())), preferred_element_type=F32
    )
    store_chunks(outs, slice(None), far)


def mirror_product(where, flex, own):
    rows, width = own.shape
    chunks = width // LANES
    tile = tile_of(rows, 1024)
    steps = rows // tile
    return pl.pallas_call(
        mirror_kernel,
        out_shape=(jax.ShapeDtypeStruct((rows, LANES), F32),) * chunks,
        grid_spec=pltpu.PrefetchScalarGridSpec(
            num_scalar_prefetch=1,
            grid=(steps,),
            in_specs=[
                pl.BlockSpec((rows, tile), lambda i, w: (0, w[1] * steps + i)),
                pl.BlockSpec((rows, width), lambda i, w: (0, 0)),
            ],
            out_specs=(pl.BlockSpec((tile, LANES), lambda i, w: (i, 0)),) * chunks,
        ),
        compiler_params=params(LIMIT),
        cost_estimate=cost(2 * rows * rows * width, 2 * rows * rows + 6 * rows * width),
        name="mirror_product",
    )(where, flex, own)


def image_kernel(where_ref, flex_ref, own_ref, came_ref, *rest):
    outs, whole_ref = rest[:-1], rest[-1]
    rows = own_ref.shape[0]
    tile = flex_ref.shape[0]
    step = pl.program_id(0)

    @pl.when(step == 0)
    def _():
        for j, ref in enumerate((own_ref, came_ref)):
            span = pl.ds(pl.multiple_of(where_ref[j] * rows, rows), rows)
            whole_ref[span, :] = masked(ref, where_ref[2 + j])

    image = jnp.dot(flex_ref[...], whole_ref[...], preferred_element_type=F32)
    ids = step * tile + lax.broadcasted_iota(jnp.int32, image.shape, 0)
    image = jnp.where(ids < where_ref[2], image, jnp.zeros_like(image))
    store_chunks(outs, slice(None), image.astype(BF16).astype(F32))


def image_product(where, flex, own, came):
    rows, width = own.shape
    chunks = width // LANES
    tile = tile_of(rows, 512)
    whole = pl.BlockSpec((rows, width), lambda i, w: (0, 0))
    return pl.pallas_call(
        image_kernel,
        out_shape=(jax.ShapeDtypeStruct((rows, LANES), F32),) * chunks,
        grid_spec=pltpu.PrefetchScalarGridSpec(
            num_scalar_prefetch=1,
            grid=(rows // tile,),
            in_specs=[pl.BlockSpec((tile, 2 * rows), lambda i, w: (i, 0)), whole, whole],
            out_specs=(pl.BlockSpec((tile, LANES), lambda i, w: (i, 0)),) * chunks,
            scratch_shapes=[pltpu.VMEM((2 * rows, width), BF16)],
        ),
        compiler_params=params(LIMIT),
        cost_estimate=cost(4 * rows * rows * width, 4 * rows * rows + 6 * rows * width),
        name="image_product",
    )(where, flex, own, came)


def pick_rows(list_ref, settled_ref, out_ref, rows_ref):
    count = out_ref.shape[0]
    group = tile_of(count, 128)

    def step(block, carry):
        first = pl.multiple_of(block * group, group)
        for k in range(group):
            source = list_ref[first + k]
            rows_ref[pl.ds(first + k, 1), :] = settled_ref[pl.ds(source, 1), :]
        return carry

    lax.fori_loop(0, count // group, step, 0)
    out_ref[...] = rows_ref[...].astype(out_ref.dtype)


def settle_kernel(list_ref, live_ref, here_ref, far_ref, came_ref, settled_ref, out_ref, rows_ref):
    rows = far_ref.shape[0]
    settled_ref[pl.ds(0, rows), :] = here_ref[...]
    grown = jnp.exp2(came_ref[pl.ds(rows, 1), :])
    there = far_ref[...] + came_ref[pl.ds(0, rows), :] * grown
    ids = lax.broadcasted_iota(jnp.int32, there.shape, 0)
    there = jnp.where(ids < live_ref[0], there, jnp.zeros_like(there))
    settled_ref[pl.ds(rows, rows), :] = there.astype(BF16).astype(F32)
    pick_rows(list_ref, settled_ref, out_ref, rows_ref)


def settle(rows_list, live, here, far, came):
    count = rows_list.shape[0]
    rows, lanes = far.shape
    return pl.pallas_call(
        settle_kernel,
        out_shape=(
            jax.ShapeDtypeStruct((2 * rows, lanes), F32),
            jax.ShapeDtypeStruct((count, lanes), BF16),
        ),
        in_specs=[SMEM, SMEM, VMEM, VMEM, VMEM],
        out_specs=(VMEM, VMEM),
        scratch_shapes=[pltpu.VMEM((count, lanes), F32)],
        compiler_params=params(20),
        cost_estimate=cost(0, 20 * rows * lanes + 2 * count * lanes),
        name="settle",
    )(rows_list, live, here, far, came)


def gather_rows(rows_list, settled):
    count = rows_list.shape[0]
    lanes = settled.shape[1]
    return pl.pallas_call(
        pick_rows,
        out_shape=jax.ShapeDtypeStruct((count, lanes), BF16),
        in_specs=[SMEM, VMEM],
        out_specs=VMEM,
        scratch_shapes=[pltpu.VMEM((count, lanes), F32)],
        compiler_params=params(8),
        cost_estimate=cost(0, 4 * settled.size + 2 * count * lanes),
        name="gather_rows",
    )(rows_list, settled)


def assemble_kernel(earlier, blocks_ref, *refs):
    tables = (refs[0:3], refs[3:6])
    settled_ref, cames = refs[6], refs[7:9]
    finished = refs[9:-8]
    out_ref, rows_refs, sums, sems = refs[-8], refs[-7:-5], refs[-5:-1], refs[-1]
    rows = settled_ref.shape[0]
    copies = []

    def send(source, first, size, chunk):
        half = rows // 2
        target = pl.multiple_of(blocks_ref[first // half] * half + first % half, size)
        copy = pltpu.make_async_copy(
            source.at[pl.ds(first, size), :],
            out_ref.at[pl.ds(target, size), pl.ds(chunk * LANES, LANES)],
            sems.at[len(copies)],
        )
        copy.start()
        copies.append(copy)

    if earlier is not None:
        for c, ref in enumerate(finished):
            for b in range(2):
                send(ref, b * (rows // 2), rows // 2, c)
    for j in range(2):
        rows_refs[j][...] = cames[j][...].astype(F32)
        sums[2 * j + 1][...] = jnp.zeros_like(settled_ref)
    sums[0][...] = settled_ref[...]
    sums[2][...] = jnp.zeros_like(settled_ref)
    count = cames[0].shape[0]
    group = tile_of(count, 128)

    def step(block, carry):
        start = pl.multiple_of(block * group, group)
        for k in range(group):
            s = start + k
            for j in range(2):
                targets_ref, places_ref, weights_ref = tables[j]
                row = targets_ref[s]
                at = places_ref[s]
                weight = weights_ref[pl.ds(s, 1), :]
                first = rows_refs[j][pl.ds(at, 1), :]
                second = rows_refs[j][pl.ds(at + 1, 1), :]
                jump = (1.0 - weight) * first + weight * second
                total = sums[2 * (k % 2) + j]
                total[pl.ds(row, 1), :] = total[pl.ds(row, 1), :] - jump
        return carry

    lax.fori_loop(0, count // group, step, 0)
    if earlier is None:
        out_ref[...] = (sums[0][...] + sums[1][...]) + (sums[2][...] + sums[3][...])
        return
    piece = rows // 8
    for q in range(8):
        span = pl.ds(q * piece, piece)
        sums[0][span, :] = (sums[0][span, :] + sums[1][span, :]) + (
            sums[2][span, :] + sums[3][span, :]
        )
        send(sums[0], q * piece, piece, earlier)
    for copy in copies:
        copy.wait()


def assemble(blocks, tables, settled, fast, slow, finished=None):
    rows = settled.shape[0]
    count = fast.shape[0]
    more = [] if finished is None else finished
    earlier = None if finished is None else len(finished)
    width = LANES if finished is None else (earlier + 1) * LANES
    return pl.pallas_call(
        lambda *refs: assemble_kernel(earlier, *refs),
        out_shape=jax.ShapeDtypeStruct((rows, width), F32),
        in_specs=[SMEM] + [SMEM, SMEM, VMEM] * 2 + [VMEM] * (3 + len(more)),
        out_specs=VMEM if finished is None else ANY,
        scratch_shapes=[pltpu.VMEM((count, LANES), F32)] * 2
        + [pltpu.VMEM((rows, LANES), F32)] * 4
        + [pltpu.SemaphoreType.DMA((8 + 2 * len(more),))],
        compiler_params=params(24),
        cost_estimate=cost(0, 8 * settled.size + 4 * fast.size),
        name="assemble",
    )(blocks, *tables[0], *tables[1], settled, fast, slow, *more)


def after(value, *earlier):
    return lax.optimization_barrier((value, *earlier))[0]


def on_device(
    multipliers, flexibility, interface_sizes, send_rows, recv_rows, recv_pos, recv_weight
):
    block = multipliers[0]
    flex = flexibility[0]
    rows, cases = block.shape
    width = cases // 2
    chunks = width // LANES
    me = lax.axis_index("panel")
    other = 1 - me
    region = lax.axis_index("region")
    regions = lax.axis_size("region")
    side = region % 2
    size = interface_sizes[0]
    swap = [(0, 1), (1, 0)]
    inner = [(r, r ^ 1) for r in range(regions)]
    outer = [(r, (r + (1 if r % 2 else -1)) % regions) for r in range(regions)]

    live_here = size - me * rows
    live_there = size - other * rows
    where = jnp.stack([me, other, live_here, live_there]).astype(jnp.int32)
    others = lax.dynamic_slice_in_dim(block, other * width, width, axis=1)
    came = lax.ppermute(others, "panel", swap)

    def local_order(index):
        return (index + me * rows) % (2 * rows)

    lists = local_order(send_rows[region])
    slow_list, fast_list = lists[side], lists[1 - side]

    recv_local = local_order(recv_rows[0])
    tables = []
    for j in (1 - side, side):
        weight = jnp.broadcast_to(recv_weight[0][j][:, None], (recv_rows.shape[2], LANES))
        tables.append((recv_local[j], recv_pos[0][j], weight))
    blocks = where[:2]
    live = live_there[None]

    own = lax.dynamic_slice_in_dim(after(block, others), me * width, width, axis=1)
    own, tables, slow_list, fast_list, blocks, live, held = lax.optimization_barrier(
        (own, tables, slow_list, fast_list, blocks, live, others)
    )
    parts = product(part_kernel, [(rows + 16, LANES)] * chunks, where, flex, held)
    payloads = []
    order = others
    for c in range(chunks):
        order = after(parts[c], order).astype(jnp.float16)
        payloads.append(lax.ppermute(order, "panel", swap))
    fars = mirror_product(where, flex, after(own, order))
    own = after(own, fars)
    heres = image_product(where, flex, own, came)

    settled, slow, fast = [], [], []
    last = heres[0]
    for c in range(chunks):
        arrived = after(payloads[c], last).astype(F32)
        whole, sent = settle(slow_list, live, heres[c], fars[c], arrived)
        slow.append(lax.ppermute(sent, "region", outer))
        last = gather_rows(after(fast_list, sent), whole)
        fast.append(lax.ppermute(last, "region", inner))
        settled.append(whole)
    blocks = after(blocks, last)
    finished = []
    for c in range(chunks - 1):
        finished.append(assemble(blocks, tables, settled[c], fast[c], slow[c]))
    result = assemble(blocks, tables, settled[-1], fast[-1], slow[-1], finished)
    return result[None]


def solution(mesh):
    assert mesh.shape["panel"] == 2 and mesh.shape["region"] % 2 == 0
    in_specs = (
        P("region", "panel", None),
        P("region", "panel", None),
        P("region"),
        P(),
        P("region", None, None),
        P("region", None, None),
        P("region", None, None),
    )
    out_specs = P("region", None, "panel")
    return jax.shard_map(
        on_device, mesh=mesh, in_specs=in_specs, out_specs=out_specs, check_vma=False
    )
```
